256 devices in a mesh: fsdp: 32 (over y, x, core), tp: 8 (over z).
Axes of the slice: x: 4, y: 4, z: 8, core: 2. Of those that a mesh axis runs over, the one named last changes fastest.
Arguments:
- dec_queries: bfloat16 [2, 64, 8192], P(None, 'fsdp', 'tp'), may hold values from -160 to 160
- cache_keys: bfloat16 [64, 4096, 1024], P('fsdp', None, 'tp'), may hold values from -5.2 to 5.2
- cached_value_rows: bfloat16 [64, 4096, 1024], P('fsdp', None, 'tp'), may hold values from -6 to 6
- step_keys: bfloat16 [2, 64, 1024], P(None, 'fsdp', 'tp'), may hold values from -6 to 6
- step_values: bfloat16 [2, 64, 1024], P(None, 'fsdp', 'tp'), may hold values from -6 to 6
- prompt_lengths: int32 [64], P('fsdp'), may hold values from 2 to 4096
- resp_embed: bfloat16 [512, 32, 8192], P('fsdp', None, 'tp'), may hold values from -520 to 520
- resp_ids: int32 [512, 32], P('fsdp'), may hold values from 0 to 152063
- resp_lengths: int32 [512], P('fsdp'), may hold values from 25 to 32
- dest_shard: int32 [512], P('fsdp'), may hold values from 0 to 31, as said below
- dest_offset: int32 [512], P('fsdp'), may hold values from 0 to 511, as said below
- norm_gain: float32 [8192], replicated, may hold values from 0.7 to 7
- w_q: bfloat16 [8192, 8192], P('fsdp', 'tp'), may hold values from -0.0625 to 0.0625
- key_value_weight: bfloat16 [8192, 2, 1024], P('fsdp', None, 'tp'), may hold values from -0.0625 to 0.0625
- bias_q: float32 [8192], P('tp'), may hold values from -3 to 3
- key_value_bias: float32 [2, 1024], P(None, 'tp'), may hold values from -3 to 3
Outputs:
- decode_out: bfloat16 [2, 64, 8192], P(None, 'fsdp', 'tp')
- packed_ids: int32 [16384], P('fsdp')
- ref_attn: bfloat16 [16384, 8192], P('fsdp', 'tp')
The draws below stay inside these ranges and needn't reach their ends.
Inputs may be any that keep to these rules, and one draw needn't show every extreme that they name: `dest_shard`: each shard receives exactly 16 responses; the 16 responses held by one index of fsdp go 1 each to half of the shards and none to the others. The responses of one shard occupy disjoint runs from dest_offset to dest_offset + resp_lengths - 1 within its 512 positions.
All inputs are finite; a program needn't handle non-finite values.
Results may differ from the reference program's by a relative error of at most 0.005.
The reference program's roundings to bfloat16 on the way count: a program that leaves them out, or rounds other values in their place, can miss the bound.
Values may be sent and summed in bfloat16 or wider, within the bound.
No kernel may reach another device: no remote copies, remote signals or barrier semaphores. Data moves between devices by JAX's collectives and lax.ppermute only.
A program may use at most 128 MiB of HBM per device.

```python
import math
import jax
import jax.numpy as jnp
from jax import lax

MODEL_WIDTH = 8192
QUERY_HEADS = 64
KEY_VALUE_HEADS = 8
HEAD_SIZE = 128
VOCAB = 152064
CACHE_SLOTS = 4096
DECODE_STEPS = 2
RLEN = 32
RESP_DEV = 16
PACKED_TOKENS = 512
NRESP = 512
PACKED = 16384
DECODE_ROWS_ALL = 64
N_FSDP = 32


def drawn_rows(key):
    leading_keys = jnp.clip(jax.random.normal(jax.random.fold_in(key, 64), (DECODE_ROWS_ALL, 1, KEY_VALUE_HEADS * HEAD_SIZE), jnp.float32), -5.0, 5.0)
    return leading_keys


def draw_cache_keys(key, part):
    leading_keys = drawn_rows(key)
    trailing_keys = jnp.clip(jax.random.normal(jax.random.fold_in(key, 65), (DECODE_ROWS_ALL, 1, KEY_VALUE_HEADS * HEAD_SIZE), jnp.float32), -5.0, 5.0)
    leftover_rows = jnp.clip(jax.random.normal(jax.random.fold_in(key, 66), (DECODE_ROWS_ALL, CACHE_SLOTS - 2, KEY_VALUE_HEADS * HEAD_SIZE), jnp.float32), -5.0, 5.0)
    return jnp.concatenate([leading_keys, trailing_keys, leftover_rows], axis=1).astype(jnp.bfloat16)


def draw_dec_queries(key, part):
    values = jnp.clip(jax.random.normal(jax.random.fold_in(key, 67), (DECODE_STEPS, DECODE_ROWS_ALL, QUERY_HEADS * HEAD_SIZE), jnp.float32), -5.0, 5.0)
    return values.astype(jnp.bfloat16)


def draw_prompt_lengths(key, part):
    lengths = jax.random.randint(jax.random.fold_in(key, 41), (DECODE_ROWS_ALL,), 2, CACHE_SLOTS + 1)
    longest = jax.random.randint(jax.random.fold_in(key, 42), (), 0, DECODE_ROWS_ALL)
    return jnp.where(jnp.arange(DECODE_ROWS_ALL) == longest, CACHE_SLOTS, lengths).astype(jnp.int32)


def routing(key):
    nshard = N_FSDP
    group_count = nshard // 2
    per_group = RESP_DEV // group_count
    resp_index = jnp.arange(NRESP, dtype=jnp.int32)
    source = resp_index // RESP_DEV
    within = resp_index % RESP_DEV
    shard_perm = jax.random.permutation(jax.random.fold_in(key, 51), nshard)
    source_perm = jax.random.permutation(jax.random.fold_in(key, 52), nshard)
    shifts = jax.random.permutation(jax.random.fold_in(key, 53), nshard)[:group_count]
    destination = shard_perm[(source_perm[source] + shifts[within // per_group]) % nshard].astype(jnp.int32)
    heavy_shard = jax.random.randint(jax.random.fold_in(key, 55), (), 0, nshard)
    spread = max(RLEN // 4, 2)
    raw_bits = jax.random.randint(jax.random.fold_in(key, 56), (NRESP,), 0, 1 << 20)
    lengths = RLEN - raw_bits % spread
    first_heavy = jnp.argmax((destination == heavy_shard).astype(jnp.int32))
    lengths = jnp.where(resp_index == first_heavy, RLEN, lengths).astype(jnp.int32)
    same_shard = destination[:, None] == destination[None, :]
    before = resp_index[None, :] < resp_index[:, None]
    offsets = jnp.sum(jnp.where(same_shard & before, lengths[None, :], 0), axis=1).astype(jnp.int32)
    return (destination, lengths, offsets)


def draw_dest_shard(key, part):
    return routing(key)[0]


def draw_resp_lengths(key, part):
    return routing(key)[1]


def draw_dest_offset(key, part):
    return routing(key)[2]


def draw_resp_embed(key, part):
    full_shape = (NRESP, RLEN, MODEL_WIDTH)
    row_scale = jnp.exp(jax.random.uniform(jax.random.fold_in(key, 31), (NRESP, RLEN, 1), jnp.float32, 0.0, math.log(10.0)))
    col_scale = jnp.exp(jax.random.uniform(jax.random.fold_in(key, 32), (1, 1, MODEL_WIDTH), jnp.float32, 0.0, math.log(10.0)))
    base_draw = jnp.clip(jax.random.normal(jax.random.fold_in(key, 33), full_shape, jnp.float32), -5.0, 5.0)
    values = base_draw * row_scale * col_scale
    return values.astype(jnp.bfloat16)


def draw_norm_gain(key, part):
    gains = 1.0 + 0.1 * jnp.clip(jax.random.normal(jax.random.fold_in(key, 71), (MODEL_WIDTH,), jnp.float32), -3.0, 3.0)
    return gains.astype(jnp.float32)


def set_ends(drawn, own_key, low, high):
    longest = drawn.shape.index(max(drawn.shape))
    spots = []
    for shift in (0, 1):
        where = [jax.random.randint(jax.random.fold_in(own_key, axis), (), 0, length) for axis, length in enumerate(drawn.shape)]
        where[longest] = (where[longest] + shift) % drawn.shape[longest]
        spots.append(tuple(where))
    return drawn.at[spots[0]].set(low).at[spots[1]].set(high)


def block_levels(key, shape, cuts, least, largest):
    gain, own = 1.0, jax.random.fold_in(key, 6)
    for dim, shards_of in cuts:
        draws = jnp.exp(jax.random.uniform(jax.random.fold_in(own, dim), (shards_of,), jnp.float32, least / len(cuts), largest / len(cuts)))
        gain = gain * jnp.repeat(draws, shape[dim] // shards_of).reshape([-1 if axis == dim else 1 for axis in range(len(shape))])
    return gain


def bell_draw(own_key, extent, width, bound, pieces=(), kind=jnp.bfloat16):
    values = width * jax.random.normal(own_key, extent, jnp.float32)
    if pieces:
        values = values * block_levels(own_key, extent, pieces, -0.22, 0.18)
    return jnp.clip(values, -bound, bound).astype(kind)


def setup_inputs(seed: int = 0) -> dict:
    key_list = jax.random.split(jax.random.key(seed), 17)
    dec_queries = draw_dec_queries(jax.random.fold_in(key_list[16], 71), 0)
    cache_keys = draw_cache_keys(jax.random.fold_in(key_list[16], 71), 0)
    cached_value_rows = bell_draw(key_list[2], (DECODE_ROWS_ALL, CACHE_SLOTS, KEY_VALUE_HEADS * HEAD_SIZE), 1.0, 6.0, ((0, 32), (2, 8)))
    step_keys = bell_draw(key_list[3], (DECODE_STEPS, DECODE_ROWS_ALL, KEY_VALUE_HEADS * HEAD_SIZE), 1.0, 6.0, ((1, 32), (2, 8)))
    step_values = bell_draw(key_list[4], (DECODE_STEPS, DECODE_ROWS_ALL, KEY_VALUE_HEADS * HEAD_SIZE), 1.0, 6.0, ((1, 32), (2, 8)))
    prompt_lengths = draw_prompt_lengths(jax.random.fold_in(key_list[16], 71), 0)
    resp_embed = draw_resp_embed(jax.random.fold_in(key_list[16], 71), 0)
    resp_ids = set_ends(jax.random.randint(key_list[7], (NRESP, RLEN), 0, VOCAB), jax.random.fold_in(key_list[7], 1), 0, VOCAB - 1).astype(jnp.int32)
    resp_lengths = draw_resp_lengths(jax.random.fold_in(key_list[16], 71), 0)
    dest_shard = draw_dest_shard(jax.random.fold_in(key_list[16], 71), 0)
    dest_offset = draw_dest_offset(jax.random.fold_in(key_list[16], 71), 0)
    norm_gain = draw_norm_gain(jax.random.fold_in(key_list[16], 71), 0)
    w_q = bell_draw(key_list[12], (MODEL_WIDTH, QUERY_HEADS * HEAD_SIZE), MODEL_WIDTH ** -0.5, 0.0625, ((0, 32), (1, 8)))
    key_value_weight = bell_draw(key_list[13], (MODEL_WIDTH, 2, KEY_VALUE_HEADS * HEAD_SIZE), MODEL_WIDTH ** -0.5, 0.0625, ((0, 32), (2, 8)))
    bias_q = bell_draw(key_list[14], (QUERY_HEADS * HEAD_SIZE,), 0.5, 3.0, ((0, 8),), jnp.float32)
    key_value_bias = bell_draw(key_list[15], (2, KEY_VALUE_HEADS * HEAD_SIZE), 0.5, 3.0, ((1, 8),), jnp.float32)
    return dict(dec_queries=dec_queries, cache_keys=cache_keys, cached_value_rows=cached_value_rows, step_keys=step_keys, step_values=step_values, prompt_lengths=prompt_lengths, resp_embed=resp_embed, resp_ids=resp_ids, resp_lengths=resp_lengths, dest_shard=dest_shard, dest_offset=dest_offset, norm_gain=norm_gain, w_q=w_q, key_value_weight=key_value_weight, bias_q=bias_q, key_value_bias=key_value_bias)


rope_base = 1000000.0
eps_norm = 1e-06

def rotate_half(values, positions):
    half_dim = HEAD_SIZE // 2
    frequency = rope_base ** (-jnp.arange(half_dim, dtype=jnp.float32) * 2.0 / HEAD_SIZE)
    angles = positions.astype(jnp.float32)[:, None] * frequency[None, :]
    cosine = jnp.cos(angles)[:, None, :]
    sine_part = jnp.sin(angles)[:, None, :]
    lower_half = values[..., :half_dim]
    upper_half = values[..., half_dim:]
    return jnp.concatenate([lower_half * cosine - upper_half * sine_part, upper_half * cosine + lower_half * sine_part], axis=-1)

def rounded(values):
    return lax.optimization_barrier(values.astype(jnp.bfloat16)).astype(jnp.float32)

def decode_row(row_inputs):
    query_rows, key_matrix, value_matrix, latest_keys, latest_values, length = row_inputs
    head_groups = QUERY_HEADS // KEY_VALUE_HEADS
    score_scale = HEAD_SIZE ** (-0.5)
    query_rows = query_rows.astype(jnp.float32).reshape(DECODE_STEPS, KEY_VALUE_HEADS, head_groups, HEAD_SIZE)
    key_matrix = key_matrix.astype(jnp.float32).reshape(CACHE_SLOTS, KEY_VALUE_HEADS, HEAD_SIZE)
    value_matrix = value_matrix.astype(jnp.float32).reshape(CACHE_SLOTS, KEY_VALUE_HEADS, HEAD_SIZE)
    latest_key = latest_keys.astype(jnp.float32).reshape(DECODE_STEPS, KEY_VALUE_HEADS, HEAD_SIZE)
    latest_value = latest_values.astype(jnp.float32).reshape(DECODE_STEPS, KEY_VALUE_HEADS, HEAD_SIZE)
    cached = jnp.einsum('skgd,ckd->skgc', query_rows, key_matrix) * score_scale
    live_mask = jnp.arange(CACHE_SLOTS, dtype=jnp.int32) < length
    cached = jnp.where(live_mask[None, None, None, :], cached, -jnp.inf)
    recent = jnp.einsum('skgd,ukd->skgu', query_rows, latest_key) * score_scale
    causal = jnp.arange(DECODE_STEPS)[None, :] <= jnp.arange(DECODE_STEPS)[:, None]
    recent = jnp.where(causal[:, None, None, :], recent, -jnp.inf)
    highest = jnp.maximum(lax.optimization_barrier(jnp.max(cached, axis=-1)), lax.optimization_barrier(jnp.max(recent, axis=-1)))[..., None]
    cached_w = jnp.exp(cached - highest)
    recent_w = jnp.exp(recent - highest)
    totals = lax.optimization_barrier(jnp.sum(cached_w, axis=-1, keepdims=True)) + lax.optimization_barrier(jnp.sum(recent_w, axis=-1, keepdims=True))
    cached_w = rounded(cached_w / totals)
    recent_w = rounded(recent_w / totals)
    output = jnp.einsum('skgc,ckd->skgd', cached_w, value_matrix) + jnp.einsum('skgu,ukd->skgd', recent_w, latest_value)
    return output.reshape(DECODE_STEPS, QUERY_HEADS * HEAD_SIZE).astype(jnp.bfloat16)

def attend_packed(query_raw, unscaled_pairs, doc_ids, token_row, covered):
    token_count = query_raw.shape[0]
    kv_count = unscaled_pairs.shape[2] // HEAD_SIZE
    head_groups = QUERY_HEADS // KEY_VALUE_HEADS
    query_rows = rounded(rotate_half(query_raw.reshape(token_count, kv_count * head_groups, HEAD_SIZE), token_row))
    key_matrix = rounded(rotate_half(unscaled_pairs[:, 0].reshape(token_count, kv_count, HEAD_SIZE), token_row))
    value_matrix = rounded(unscaled_pairs[:, 1].reshape(token_count, kv_count, HEAD_SIZE))
    query_rows = query_rows.reshape(token_count, kv_count, head_groups, HEAD_SIZE)
    scores = jnp.einsum('tkgd,skd->kgts', query_rows, key_matrix) * HEAD_SIZE ** (-0.5)
    indices = jnp.arange(token_count, dtype=jnp.int32)
    allowed = (doc_ids[:, None] == doc_ids[None, :]) & (indices[None, :] <= indices[:, None])
    scores = jnp.where(allowed, scores, -jnp.inf)
    highest = lax.optimization_barrier(jnp.max(scores, axis=-1, keepdims=True))
    weights = jnp.exp(scores - highest)
    weights = rounded(weights / lax.optimization_barrier(jnp.sum(weights, axis=-1, keepdims=True)))
    output = jnp.einsum('kgts,skd->tkgd', weights, value_matrix)
    output = jnp.where(covered[:, None, None, None], output, 0.0)
    return output.reshape(token_count, kv_count * head_groups * HEAD_SIZE).astype(jnp.bfloat16)

def reference(dec_queries, cache_keys, cached_value_rows, step_keys, step_values, prompt_lengths, resp_embed, resp_ids, resp_lengths, dest_shard, dest_offset, norm_gain, w_q, key_value_weight, bias_q, key_value_bias):
    decode_out = lax.map(decode_row, (jnp.swapaxes(dec_queries, 0, 1), cache_keys, cached_value_rows, jnp.swapaxes(step_keys, 0, 1), jnp.swapaxes(step_values, 0, 1), prompt_lengths))
    decode_out = jnp.swapaxes(decode_out, 0, 1)
    flattened_weight = key_value_weight.reshape(MODEL_WIDTH, 2 * KEY_VALUE_HEADS * HEAD_SIZE)
    resp_index = jnp.arange(NRESP, dtype=jnp.int32)
    resp_end = dest_offset + resp_lengths

    def shard_pass(shard_idx):
        position = jnp.arange(PACKED_TOKENS, dtype=jnp.int32)
        inside = (dest_shard[None, :] == shard_idx) & (position[:, None] >= dest_offset[None, :]) & (position[:, None] < resp_end[None, :])
        covered = jnp.any(inside, axis=1)
        resp_pick = lax.optimization_barrier(jnp.sum(jnp.where(inside, resp_index[None, :], 0), axis=1)).astype(jnp.int32)
        token_row = (position - lax.optimization_barrier(jnp.sum(jnp.where(inside, dest_offset[None, :], 0), axis=1))).astype(jnp.int32)
        token_row = jnp.where(covered, token_row, 0).astype(jnp.int32)
        tokens = jnp.where(covered[:, None], resp_embed[resp_pick, token_row], jnp.zeros((), jnp.bfloat16))
        shard_ids = jnp.where(covered, resp_ids[resp_pick, token_row], -1).astype(jnp.int32)
        doc_ids = jnp.where(covered, resp_pick, -1).astype(jnp.int32)
        wide = tokens.astype(jnp.float32)
        scaled_input = (wide * lax.rsqrt(lax.optimization_barrier(jnp.mean(wide * wide, axis=1, keepdims=True)) + eps_norm) * norm_gain[None, :]).astype(jnp.bfloat16)
        query_raw = jnp.dot(scaled_input, w_q, preferred_element_type=jnp.float32) + bias_q[None, :]
        unscaled_pairs = jnp.dot(scaled_input, flattened_weight, preferred_element_type=jnp.float32).reshape(PACKED_TOKENS, 2, KEY_VALUE_HEADS * HEAD_SIZE) + key_value_bias[None]
        attention = attend_packed(query_raw, unscaled_pairs, doc_ids, token_row, covered)
        return (shard_ids, attention)
    packed_ids, ref_attn = lax.map(shard_pass, jnp.arange(N_FSDP, dtype=jnp.int32))
    return (decode_out, packed_ids.reshape(PACKED), ref_attn.reshape(PACKED, QUERY_HEADS * HEAD_SIZE))
```

```python
import functools
import jax
import jax.numpy as jnp
from jax import lax
from jax.experimental import pallas as pl
from jax.experimental.pallas import tpu as pltpu
from jax.sharding import PartitionSpec as P

QUERY_HEADS = 64
KEY_VALUE_HEADS = 8
HEAD_SIZE = 128
GROUPS = QUERY_HEADS // KEY_VALUE_HEADS

rope_base = 1000000.0
eps_norm = 1e-06


def decode_local(
    dec_queries, cache_keys, cached_value_rows, step_keys, step_values, prompt_lengths
):
    step_count, row_count, head_width = dec_queries.shape
    head_groups = QUERY_HEADS // KEY_VALUE_HEADS
    kv_local = cache_keys.shape[2] // HEAD_SIZE
    length = cache_keys.shape[1]
    score_scale = HEAD_SIZE ** (-0.5)
    query_rows = dec_queries.reshape(step_count, row_count, kv_local, head_groups, HEAD_SIZE)
    key_matrix = cache_keys.reshape(row_count, length, kv_local, HEAD_SIZE)
    value_matrix = cached_value_rows.reshape(row_count, length, kv_local, HEAD_SIZE)
    latest_key = step_keys.reshape(step_count, row_count, kv_local, HEAD_SIZE)
    latest_value = step_values.reshape(step_count, row_count, kv_local, HEAD_SIZE)
    cached = (
        jnp.einsum("srkgd,rckd->srkgc", query_rows, key_matrix, preferred_element_type=jnp.float32)
        * score_scale
    )
    live_mask = jnp.arange(length, dtype=jnp.int32)[None, :] < prompt_lengths[:, None]
    cached = jnp.where(live_mask[None, :, None, None, :], cached, -jnp.inf)
    recent = (
        jnp.einsum("srkgd,urkd->srkgu", query_rows, latest_key, preferred_element_type=jnp.float32)
        * score_scale
    )
    causal = jnp.arange(step_count)[None, :] <= jnp.arange(step_count)[:, None]
    recent = jnp.where(causal[:, None, None, None, :], recent, -jnp.inf)
    highest = jnp.maximum(jnp.max(cached, axis=-1), jnp.max(recent, axis=-1))[..., None]
    cached_w = jnp.exp(cached - highest)
    recent_w = jnp.exp(recent - highest)
    totals = jnp.sum(cached_w, axis=-1, keepdims=True) + jnp.sum(recent_w, axis=-1, keepdims=True)
    cached_w = (cached_w / totals).astype(jnp.bfloat16)
    recent_w = (recent_w / totals).astype(jnp.bfloat16)
    output = jnp.einsum(
        "srkgc,rckd->srkgd", cached_w, value_matrix, preferred_element_type=jnp.float32
    )
    output = output + jnp.einsum(
        "srkgu,urkd->srkgd", recent_w, latest_value, preferred_element_type=jnp.float32
    )
    return output.reshape(step_count, row_count, head_width).astype(jnp.bfloat16)


def ring_shift(axis, shift):
    n = lax.axis_size(axis)
    return [(i, (i + shift) % n) for i in range(n)]


def features_around(pieces):
    up, down = ring_shift("tp", 1), ring_shift("tp", -1)
    steps = lax.axis_size("tp") // 2 - 1
    chains = [([rows], [rows]) for rows in pieces]
    for _ in range(steps):
        for ahead, behind in chains:
            ahead.append(lax.ppermute(ahead[-1], "tp", up))
            behind.append(lax.ppermute(behind[-1], "tp", down))
    near, far = [], []
    for ahead, behind in chains:
        half = ahead[0].shape[0] // 2
        near.append((ahead[1:], behind[1:]))
        far.append(
            (
                lax.ppermute(ahead[-1][:half], "tp", up),
                lax.ppermute(behind[-1][half:], "tp", down),
            )
        )
    return near, far


def project_body(
    counts, final, place_ref, dest_ref, *refs
):
    steps, parts = counts
    at = steps * parts
    x_refs = refs[:at]
    w_ref, r_ref, g_ref = refs[at : at + 3]
    at += 3
    if final:
        acc_in, bias_ref, cos_ref, sin_ref, slots_ref = refs[at : at + 5]
        at += 5
    else:
        acc_ref = refs[at]
        at += 1
    x_buf, w_buf, x_sem, w_sem = refs[at : at + 4]
    at += 4
    if final:
        acc_ref, load_sem, q_buf, out_buf, out_sem = refs[at : at + 5]
    rows, depth = x_buf.shape[1:]
    width = w_buf.shape[2]

    def x_copies(step, slot):
        part = rows // parts
        return [
            pltpu.make_async_copy(
                x_refs[step * parts + j],
                x_buf.at[slot, pl.ds(j * part, part)],
                x_sem.at[slot, j],
            )
            for j in range(parts)
        ]

    def w_copy(step, slot):
        return pltpu.make_async_copy(
            w_ref.at[pl.ds(pl.multiple_of(place_ref[step] * depth, depth), depth)],
            w_buf.at[slot],
            w_sem.at[slot],
        )

    def start(step, slot):
        w_copy(step, slot).start()
        for k in range(steps):
            @pl.when(step == k)
            def _():
                for c in x_copies(k, slot):
                    c.start()

    start(0, 0)
    if final:
        load = pltpu.make_async_copy(acc_in, acc_ref, load_sem)
        load.start()
        load.wait()
    else:
        acc_ref[...] = jnp.zeros_like(acc_ref)

    def step_body(step, carry):
        slot = lax.rem(step, 2)

        @pl.when(step + 1 < steps)
        def _():
            start(step + 1, 1 - slot)

        for c in x_copies(0, slot):
            c.wait()
        w_copy(step, slot).wait()
        gain = g_ref[pl.ds(place_ref[step], 1), :]
        normed = (x_buf[slot].astype(jnp.float32) * r_ref[...] * gain).astype(jnp.bfloat16)
        x_buf[slot] = normed

        def columns(j, carry):
            cols = pl.ds(pl.multiple_of(j * 256, 256), 256)
            acc_ref[:, cols] += jnp.dot(
                x_buf[slot], w_buf[slot, :, cols], preferred_element_type=jnp.float32
            )
            return carry

        lax.fori_loop(0, width // 256, columns, 0)
        return carry

    lax.fori_loop(0, steps, step_body, 0)
    if not final:
        return

    heads = GROUPS
    cos, sin = cos_ref[...], sin_ref[...]
    group = 4 * 32

    def rotate(x, cos, sin):
        return (x * cos + pltpu.roll(x, HEAD_SIZE // 2, 1) * sin).astype(jnp.bfloat16)

    row = lax.broadcasted_iota(jnp.int32, (group, group), 0)
    col = lax.broadcasted_iota(jnp.int32, (group, group), 1)
    allowed = (row // 32 == col // 32) & (col <= row)

    def attend(g, carry):
        at_rows = pl.ds(pl.multiple_of(g * group, group), group)
        k0 = heads * HEAD_SIZE
        keys = rotate(
            acc_ref[at_rows, k0 : k0 + HEAD_SIZE] + bias_ref[:, k0 : k0 + HEAD_SIZE],
            cos,
            sin,
        )
        v0 = k0 + HEAD_SIZE
        values = (
            acc_ref[at_rows, v0 : v0 + HEAD_SIZE] + bias_ref[:, v0 : v0 + HEAD_SIZE]
        ).astype(jnp.bfloat16)
        for h in range(heads):
            cols = slice(h * HEAD_SIZE, (h + 1) * HEAD_SIZE)
            q = rotate(acc_ref[at_rows, cols] + bias_ref[:, cols], cos, sin)
            scores = lax.dot_general(
                q, keys, (((1,), (1,)), ((), ())), preferred_element_type=jnp.float32
            ) * HEAD_SIZE ** (-0.5)
            scores = jnp.where(allowed, scores, -jnp.inf)
            weights = jnp.exp(scores - jnp.max(scores, axis=-1, keepdims=True))
            weights = (weights / jnp.sum(weights, axis=-1, keepdims=True)).astype(jnp.bfloat16)
            out = jnp.dot(weights, values, preferred_element_type=jnp.float32)
            out_buf[pl.ds(g * 4, 4), :, cols] = out.astype(jnp.bfloat16).reshape(4, 32, HEAD_SIZE)
        for j in range(4):
            n = g * 4 + j
            pltpu.make_async_copy(
                out_buf.at[n], slots_ref.at[dest_ref[n]], out_sem.at[n]
            ).start()
        return carry

    lax.fori_loop(0, rows // group, attend, 0)
    for n in range(rows // 32):
        pltpu.make_async_copy(out_buf.at[n], slots_ref.at[0], out_sem.at[n]).wait()


def project(x_steps, places, dest, weight, scale, gain, acc=None, bias=None, cos=None, sin=None):
    steps, parts = len(x_steps), len(x_steps[0])
    rows = scale.shape[0]
    depth = x_steps[0][0].shape[1]
    width = weight.shape[1]
    final = acc is not None
    any_spec = pl.BlockSpec(memory_space=pl.ANY)
    vmem = pl.BlockSpec(memory_space=pltpu.VMEM)
    smem = pl.BlockSpec(memory_space=pltpu.SMEM)
    flat = [a for s in x_steps for a in s]
    args = [places, dest] + flat + [weight, scale, gain]
    in_specs = [smem, smem] + [any_spec] * (len(flat) + 1) + [vmem, vmem]
    scratch = [
        pltpu.VMEM((2, rows, depth), jnp.bfloat16),
        pltpu.VMEM((2, depth, width), jnp.bfloat16),
        pltpu.SemaphoreType.DMA((2, parts)),
        pltpu.SemaphoreType.DMA((2,)),
    ]
    flops = 2 * rows * depth * width * steps
    moved = steps * (rows * depth + depth * width) * 2 + rows * width * 4
    if final:
        args += [acc, bias, cos, sin]
        in_specs += [any_spec, vmem, vmem, vmem]
        out_shape = jax.ShapeDtypeStruct((32, 32, GROUPS * HEAD_SIZE), jnp.bfloat16)
        out_spec = any_spec
        scratch += [
            pltpu.VMEM((rows, width), jnp.float32),
            pltpu.SemaphoreType.DMA(()),
            pltpu.VMEM((8, 128), jnp.bfloat16),
            pltpu.VMEM((rows // 32, 32, GROUPS * HEAD_SIZE), jnp.bfloat16),
            pltpu.SemaphoreType.DMA((rows // 32,)),
        ]
    else:
        out_shape = jax.ShapeDtypeStruct((rows, width), jnp.float32)
        out_spec = vmem
    return pl.pallas_call(
        functools.partial(project_body, (steps, parts), final),
        out_shape=out_shape,
        in_specs=in_specs,
        out_specs=out_spec,
        scratch_shapes=scratch,
        compiler_params=pltpu.CompilerParams(vmem_limit_bytes=48 * 2**20),
        cost_estimate=pl.CostEstimate(flops=flops, bytes_accessed=moved, transcendentals=0),
    )(*args)


def pack_body(source_ref, row_ref, arrived_ref, out_ref, buf, sem):
    count = buf.shape[0]

    def copy(c):
        return pltpu.make_async_copy(arrived_ref.at[source_ref[c]], buf.at[c], sem.at[c])

    for c in range(count):
        copy(c).start()
    for c in range(count):
        copy(c).wait()
    rows = out_ref.shape[0]
    slots = buf[...].reshape(count * buf.shape[1], buf.shape[2])
    pick = (
        row_ref[...] == lax.broadcasted_iota(jnp.int32, (rows, slots.shape[0]), 1)
    ).astype(jnp.bfloat16)
    out_ref[...] = jnp.dot(pick, slots, preferred_element_type=jnp.float32).astype(jnp.bfloat16)


def pack(source, row, arrived):
    rows, width = row.shape[0], arrived.shape[2]
    vmem = pl.BlockSpec(memory_space=pltpu.VMEM)
    return pl.pallas_call(
        pack_body,
        out_shape=jax.ShapeDtypeStruct((rows, width), jnp.bfloat16),
        in_specs=[
            pl.BlockSpec(memory_space=pltpu.SMEM),
            vmem,
            pl.BlockSpec(memory_space=pl.ANY),
        ],
        out_specs=vmem,
        scratch_shapes=[
            pltpu.VMEM((16, arrived.shape[1], width), jnp.bfloat16),
            pltpu.SemaphoreType.DMA((16,)),
        ],
        compiler_params=pltpu.CompilerParams(vmem_limit_bytes=32 * 2**20),
        cost_estimate=pl.CostEstimate(
            flops=2 * rows * rows * width, bytes_accessed=4 * rows * width, transcendentals=0
        ),
    )(source, row, arrived)


def on_device(
    dec_queries,
    cache_keys,
    cached_value_rows,
    step_keys,
    step_values,
    prompt_lengths,
    resp_embed,
    resp_ids,
    resp_lengths,
    dest_shard,
    dest_offset,
    norm_gain,
    w_q,
    key_value_weight,
    bias_q,
    key_value_bias,
):
    nshard = lax.axis_size("fsdp")
    tp_size = lax.axis_size("tp")
    me = lax.axis_index("tp")
    resp_count, resp_span, depth = resp_embed.shape
    packed_len = resp_count * resp_span
    rows = resp_embed.reshape(packed_len, depth)

    near, far = features_around([rows[: packed_len // 2], rows[packed_len // 2 :]])
    w_pairs = key_value_weight.reshape(key_value_weight.shape[0], -1)
    weight = lax.all_gather(
        jnp.concatenate([w_q, w_pairs], axis=1), "fsdp", axis=0, tiled=True
    )

    wide = rows.astype(jnp.float32)
    squares = jnp.sum(wide * wide, axis=1)
    squares = lax.all_to_all(
        jnp.broadcast_to(squares[None], (tp_size, packed_len)), "tp", 0, 0, tiled=True
    )
    scale = lax.rsqrt(jnp.sum(squares, axis=0) / (depth * tp_size) + eps_norm)[:, None]

    placing = dest_shard[:, None] == jnp.arange(nshard, dtype=jnp.int32)[None, :]
    sent = jnp.concatenate(
        [resp_ids, resp_lengths[:, None], dest_offset[:, None]], axis=1
    )
    slot_meta = jnp.sum(jnp.where(placing[:, :, None], sent[:, None, :], 0), axis=0)
    arrived_meta = lax.all_to_all(slot_meta, "fsdp", split_axis=0, concat_axis=0, tiled=True)
    lengths_in = arrived_meta[:, resp_span]
    offsets_in = arrived_meta[:, resp_span + 1]
    flat_ids = arrived_meta[:, :resp_span].reshape(nshard * resp_span)
    valid = lengths_in > 0
    slot = jnp.arange(nshard, dtype=jnp.int32)
    rank = jnp.sum((valid[None, :] & (slot[None, :] < slot[:, None])).astype(jnp.int32), axis=1)
    source = jnp.sum(
        jnp.where(
            valid[None, :] & (rank[None, :] == jnp.arange(resp_count, dtype=jnp.int32)[:, None]),
            slot[None, :],
            0,
        ),
        axis=1,
    )
    position = jnp.arange(packed_len, dtype=jnp.int32)
    inside = (position[:, None] >= offsets_in[None, :]) & (
        position[:, None] < (offsets_in + lengths_in)[None, :]
    )
    covered = jnp.any(inside, axis=1)
    full_row = jnp.sum(
        jnp.where(
            inside, slot[None, :] * resp_span + position[:, None] - offsets_in[None, :], 0
        ),
        axis=1,
    )
    packed_ids = jnp.where(covered, flat_ids[full_row], -1).astype(jnp.int32)
    dense_row = jnp.sum(
        jnp.where(
            inside, rank[None, :] * resp_span + position[:, None] - offsets_in[None, :], 0
        ),
        axis=1,
    )
    dense_row = jnp.where(covered, dense_row, -1)[:, None]

    decode_out = decode_local(
        dec_queries, cache_keys, cached_value_rows, step_keys, step_values, prompt_lengths
    )

    half_dim = HEAD_SIZE // 2
    frequency = rope_base ** (-jnp.arange(half_dim, dtype=jnp.float32) * 2.0 / HEAD_SIZE)
    angles = jnp.arange(resp_span, dtype=jnp.int32).astype(jnp.float32)[:, None] * frequency[None]
    cosine, sine = jnp.cos(angles), jnp.sin(angles)
    cos = jnp.tile(jnp.concatenate([cosine, cosine], axis=1), (4, 1))
    sin = jnp.tile(jnp.concatenate([-sine, sine], axis=1), (4, 1))
    bias = jnp.concatenate([bias_q, key_value_bias[0], key_value_bias[1]])[None]
    gain = norm_gain.reshape(tp_size, depth)

    steps, places = [[rows[: packed_len // 2], rows[packed_len // 2 :]]], [me]
    for k in range(tp_size // 2 - 1):
        steps.append([n[0][k] for n in near])
        places.append((me - k - 1) % tp_size)
        steps.append([n[1][k] for n in near])
        places.append((me + k + 1) % tp_size)
    acc = project(steps, jnp.stack(places), dest_shard, weight, scale, gain)
    last = [[part for pair in far for part in pair]]
    slots = project(
        last,
        ((me + tp_size // 2) % tp_size)[None],
        dest_shard,
        weight,
        scale,
        gain,
        acc,
        bias,
        cos,
        sin,
    )
    arrived = lax.all_to_all(slots, "fsdp", split_axis=0, concat_axis=0, tiled=True)
    ref_attn = pack(source, dense_row, arrived)
    return (decode_out, packed_ids, ref_attn)


def solution(mesh):
    in_specs = (
        P(None, "fsdp", "tp"),
        P("fsdp", None, "tp"),
        P("fsdp", None, "tp"),
        P(None, "fsdp", "tp"),
        P(None, "fsdp", "tp"),
        P("fsdp"),
        P("fsdp", None, "tp"),
        P("fsdp", None),
        P("fsdp"),
        P("fsdp"),
        P("fsdp"),
        P(),
        P("fsdp", "tp"),
        P("fsdp", None, "tp"),
        P("tp"),
        P(None, "tp"),
    )
    out_specs = (P(None, "fsdp", "tp"), P("fsdp"), P("fsdp", "tp"))
    return jax.shard_map(
        on_device, mesh=mesh, in_specs=in_specs, out_specs=out_specs, check_vma=False
    )
```
